32 devices in a mesh: groups: 2 (over y), hours: 4 (over z), years: 2 (over x), lines: 2 (over core).
Axes of the slice: x: 2, y: 2, z: 4, core: 2. Of those that a mesh axis runs over, the one named last changes fastest.
Arguments:
- demand: bfloat16 [8, 4, 2048], P(('groups', 'years'), 'hours'), parts along dimension 0, may hold values from 0.19921875 to 0.796875
- avail: bfloat16 [8, 4, 4096], P(('groups', 'years'), 'hours', 'lines'), parts along dimension 0, may hold values from 0.099609375 to 1
- ptdf: bfloat16 [1536, 2048], P('lines'), may hold values from -0.125 to 0.125
- line_limit: float32 [1536], P('lines'), may hold values from 0.3 to 3
- gen_cost: float32 [4096], P('lines'), may hold values from 0.2 to 5
- gen_cap: float32 [4096], P('lines'), may hold values from 0.3 to 1.5
- gen_node: int32 [4096], P('lines'), may hold values from 0 to 2047
- store_node: int32 [8192], P('lines'), may hold values from 0 to 2047
- store_power: float32 [8192], P('lines'), may hold values from 0.2 to 1
- capex: float32 [8192], P('lines'), may hold values from 0.05 to 1
- gen_state: float32 [8, 4, 4096], P(('groups', 'years'), 'hours', 'lines'), parts along dimension 0, may hold values from 0 to 0.6
- store_state: float32 [8, 4, 8192], P(('groups', 'years'), 'hours', 'lines'), parts along dimension 0, may hold values from -0.5 to 0.5
- level_upper: float32 [8, 4, 8192], P(('groups', 'years'), 'hours', 'lines'), parts along dimension 0, may hold values from 0 to 9, as said below
- level_lower: float32 [8, 4, 8192], P(('groups', 'years'), 'hours', 'lines'), parts along dimension 0, may hold values from 0 to 0.5
- flow_dual: float32 [8, 4, 1536], P(('groups', 'years'), 'hours', 'lines'), parts along dimension 0, may hold values from -3 to 3
- balance_dual: float32 [8, 4], P(('groups', 'years'), 'hours'), parts along dimension 0, may hold values from -6 to 6
- capacity: float32 [16384], P(('groups', 'lines')), parts along dimension 0, may hold values from 0.05 to 2
Outputs:
- gen_next: float32 [8, 4, 4096], P(('groups', 'years'), 'hours', 'lines'), parts along dimension 0
- store_next: float32 [8, 4, 8192], P(('groups', 'years'), 'hours', 'lines'), parts along dimension 0
- capacity_next: float32 [16384], P(('groups', 'lines')), parts along dimension 0
- balance_next: float32 [8, 4], P(('groups', 'years'), 'hours'), parts along dimension 0
- flow_next: float32 [8, 4, 1536], P(('groups', 'years'), 'hours', 'lines'), parts along dimension 0
- upper_next: float32 [8, 4, 8192], P(('groups', 'years'), 'hours', 'lines'), parts along dimension 0
- lower_next: float32 [8, 4, 8192], P(('groups', 'years'), 'hours', 'lines'), parts along dimension 0
The draws below stay inside these ranges and needn't reach their ends.
There are 2 independent parts, one for each index of `groups`. The reference program is written for one: setup_inputs(seed, part) draws one part's arguments, and reference() takes and returns one part's arrays. A program takes and returns all parts, laid end to end along the dimension named above; an argument that names none is the same for every part. Nothing has to cross between parts.
Inputs may be any that keep to these rules, and one draw needn't show every extreme that they name: `level_upper`: nonnegative.
All inputs are finite; a program needn't handle non-finite values.
Results may differ from the reference program's by a relative error of at most 0.004.
Values may be sent and summed in bfloat16 or wider, within the bound.
A program may use at most 64 MiB of HBM per device.

```python
import math
import jax
import jax.numpy as jnp
from jax import lax

NODES = 2048
LINES = 1536
STORAGES = 8192
GENS = 4096
ITERS = 1
YEARS = 4
HOURS = 4


def draw_level_upper(key, part):
    first, second, third = jax.random.split(jax.random.fold_in(key, 11), 3)
    uniform_part = jax.random.uniform(first, (YEARS, HOURS, STORAGES), jnp.float32)
    row_scale = jnp.exp(jax.random.uniform(second, (YEARS, HOURS, 1), jnp.float32, jnp.log(0.1), 0.0))
    rising = 1.0 + 2.0 * jnp.arange(HOURS, dtype=jnp.float32)[None, :, None] / (HOURS - 1)
    column_scale = jnp.exp(jax.random.uniform(third, (1, 1, STORAGES), jnp.float32, jnp.log(0.5), jnp.log(2.0)))
    return uniform_part * row_scale * rising * column_scale


def place_ends(result, own_key, low, largest):
    index_at = [jax.random.randint(jax.random.fold_in(own_key, axis), (), 0, length) for axis, length in enumerate(result.shape)]
    longest = result.shape.index(max(result.shape))
    neighbour = index_at[:longest] + [(index_at[longest] + 1) % result.shape[longest]] + index_at[longest + 1:]
    return result.at[tuple(index_at)].set(low).at[tuple(neighbour)].set(largest)


def levels(own_key, extent, cuts, low, largest):
    loudness, own = 1.0, jax.random.fold_in(own_key, 6)
    for position, blocks in cuts:
        heights = jnp.exp(jax.random.uniform(jax.random.fold_in(own, position), (blocks,), jnp.float32, low / len(cuts), largest / len(cuts)))
        loudness = loudness * jnp.repeat(heights, extent[position] // blocks).reshape([-1 if axis == position else 1 for axis in range(len(extent))])
    return loudness


def centred(stream_key, dims, spread, bound, shards=(), held_as=jnp.bfloat16):
    gain = levels(stream_key, dims, shards, -0.22, 0.18) if shards else 1.0
    entries = jax.random.normal(stream_key, dims, jnp.float32) * spread * gain
    return jnp.minimum(jnp.maximum(entries, -bound), bound).astype(held_as)


def setup_inputs(seed: int = 0, part: int = 0) -> dict:
    arg_keys = jax.random.split(jax.random.key(seed), 18)
    part_splits = jax.random.split(jax.random.fold_in(arg_keys[17], part), 18)
    return {
        "demand": jnp.clip(0.19921875 + 0.59765625 * jax.random.uniform(part_splits[0], (YEARS, HOURS, NODES), jnp.float32) ** levels(part_splits[0], (YEARS, HOURS, NODES), ((0, 2), (1, 4)), -0.2, 0.2), 0.19921875, 0.796875).astype(jnp.bfloat16),
        "avail": jnp.clip(0.099609375 + 0.9003906 * jax.random.uniform(part_splits[1], (YEARS, HOURS, GENS), jnp.float32) ** levels(part_splits[1], (YEARS, HOURS, GENS), ((0, 2), (1, 4), (2, 2)), -0.2, 0.2), 0.099609375, 1.0).astype(jnp.bfloat16),
        "ptdf": centred(arg_keys[2], (LINES, NODES), NODES ** -0.5, 0.125, ((0, 2),)),
        "line_limit": jnp.clip(jnp.exp(math.log(3.0) - 2.3025851 * jax.random.uniform(arg_keys[3], (LINES,), jnp.float32) ** levels(arg_keys[3], (LINES,), ((0, 2),), -0.2, 0.2)), 0.3, 3.0),
        "gen_cost": jnp.clip(jnp.exp(math.log(5.0) - 3.218876 * jax.random.uniform(arg_keys[4], (GENS,), jnp.float32) ** levels(arg_keys[4], (GENS,), ((0, 2),), -0.2, 0.2)), 0.2, 5.0),
        "gen_cap": jnp.clip(jnp.exp(math.log(1.5) - 1.60943787 * jax.random.uniform(arg_keys[5], (GENS,), jnp.float32) ** levels(arg_keys[5], (GENS,), ((0, 2),), -0.2, 0.2)), 0.3, 1.5),
        "gen_node": place_ends(jax.random.randint(arg_keys[6], (GENS,), 0, NODES), jax.random.fold_in(arg_keys[6], 1), 0, NODES - 1).astype(jnp.int32),
        "store_node": place_ends(jax.random.randint(arg_keys[7], (STORAGES,), 0, NODES), jax.random.fold_in(arg_keys[7], 1), 0, NODES - 1).astype(jnp.int32),
        "store_power": jnp.clip(jnp.exp(math.log(1.0) - 1.609438 * jax.random.uniform(arg_keys[8], (STORAGES,), jnp.float32) ** levels(arg_keys[8], (STORAGES,), ((0, 2),), -0.2, 0.2)), 0.2, 1.0),
        "capex": jnp.clip(jnp.exp(math.log(1.0) - 2.9957323 * jax.random.uniform(arg_keys[9], (STORAGES,), jnp.float32) ** levels(arg_keys[9], (STORAGES,), ((0, 2),), -0.2, 0.2)), 0.05, 1.0),
        "gen_state": jnp.clip(0.6 * jax.random.uniform(part_splits[10], (YEARS, HOURS, GENS), jnp.float32) ** levels(part_splits[10], (YEARS, HOURS, GENS), ((0, 2), (1, 4), (2, 2)), -0.2, 0.2), 0.0, 0.6),
        "store_state": jnp.clip(jax.random.uniform(part_splits[11], (YEARS, HOURS, STORAGES), jnp.float32, -0.5, 0.5) * levels(part_splits[11], (YEARS, HOURS, STORAGES), ((0, 2), (1, 4), (2, 2)), -0.4, 0.0), -0.5, 0.5),
        "level_upper": draw_level_upper(jax.random.fold_in(jax.random.fold_in(arg_keys[17], part), 71), part),
        "level_lower": jnp.clip(0.5 * jax.random.uniform(part_splits[13], (YEARS, HOURS, STORAGES), jnp.float32) ** levels(part_splits[13], (YEARS, HOURS, STORAGES), ((0, 2), (1, 4), (2, 2)), -0.2, 0.2), 0.0, 0.5),
        "flow_dual": centred(part_splits[14], (YEARS, HOURS, LINES), 0.5, 3.0, ((0, 2), (1, 4), (2, 2)), jnp.float32),
        "balance_dual": centred(part_splits[15], (YEARS, HOURS), 1.0, 6.0, ((0, 2), (1, 4)), jnp.float32),
        "capacity": jnp.clip(jnp.exp(math.log(2.0) - 3.6888794 * jax.random.uniform(part_splits[16], (STORAGES,), jnp.float32) ** levels(part_splits[16], (STORAGES,), ((0, 2),), -0.2, 0.2)), 0.05, 2.0),
    }


TAU = 0.1
SIGMA = 0.5
TAU_CAP = 1.0

def reference(demand, avail, ptdf, line_limit, gen_cost, gen_cap, gen_node, store_node, store_power, capex, gen_state, store_state, level_upper, level_lower, flow_dual, balance_dual, capacity):
    level_scale = 1.0 / math.sqrt(HOURS)
    node_scale = 1.0 / math.sqrt(NODES)
    hour_count = YEARS * HOURS
    demand_full = demand.astype(jnp.float32)
    gen_limit = gen_cap * avail.astype(jnp.float32)
    dispatch, storage, capacity_now = (gen_state, store_state, capacity)
    upper, lower, line_dual, balance = (level_upper, level_lower, flow_dual, balance_dual)
    for iteration in range(ITERS):
        dual_half = line_dual.astype(jnp.bfloat16).reshape(YEARS * HOURS, LINES)
        network = jnp.dot(dual_half, ptdf, preferred_element_type=jnp.float32).reshape(YEARS, HOURS, NODES)
        prices = node_scale * balance[:, :, None] + network
        dispatch_next = jnp.clip(dispatch - TAU * (gen_cost + prices[:, :, gen_node]), 0.0, gen_limit)
        suffix = level_scale * lax.cumsum(upper - lower, axis=1, reverse=True)
        storage_next = jnp.clip(storage - TAU * (suffix - prices[:, :, store_node]), -store_power, store_power)
        upper_total = lax.optimization_barrier(jnp.sum(upper, axis=(0, 1)))
        capacity_next = jnp.maximum(capacity_now - TAU_CAP * (capex - upper_total / hour_count), 0.0)
        dispatch_bar = 2.0 * dispatch_next - dispatch
        storage_bar = 2.0 * storage_next - storage
        capacity_bar = 2.0 * capacity_next - capacity_now
        empty = jnp.zeros((YEARS, HOURS, NODES), jnp.float32)
        inject = empty.at[:, :, gen_node].add(dispatch_bar).at[:, :, store_node].add(-storage_bar) - demand_full
        balance = balance + SIGMA * node_scale * lax.optimization_barrier(jnp.sum(inject, axis=2))
        inject_half = inject.astype(jnp.bfloat16).reshape(YEARS * HOURS, NODES)
        line_flows = jnp.dot(inject_half, ptdf.T, preferred_element_type=jnp.float32).reshape(YEARS, HOURS, LINES)
        shifted = line_dual + SIGMA * line_flows
        line_dual = shifted - SIGMA * jnp.clip(shifted / SIGMA, -line_limit, line_limit)
        level = level_scale * lax.cumsum(storage_bar, axis=1)
        upper = jnp.maximum(upper + SIGMA * (level - capacity_bar), 0.0)
        lower = jnp.maximum(lower - SIGMA * level, 0.0)
        dispatch, storage, capacity_now = (dispatch_next, storage_next, capacity_next)
    return (dispatch, storage, capacity_now, balance, line_dual, upper, lower)
```

```python
import functools
import math

import jax
import jax.numpy as jnp
from jax import lax
from jax.experimental import pallas as pl
from jax.experimental.pallas import tpu as pltpu
from jax.sharding import PartitionSpec as P

TAU = 0.1
SIGMA = 0.5
TAU_CAP = 1.0
LANES = 128
SPLITS = 3
LINK = jnp.float32
MESH = pl.DeviceIdType.MESH


def step_kernel(
    sizes,
    demand_h, avail_h, ptdf_h, limit_h, cost_h, cap_h, gnode_h, snode_h, power_h,
    capex_h, gen_h, store_h, upper_h, lower_h, flow_h, capacity_h, balance_s,
    gen_o, store_o, capacity_o, flow_o, upper_o, lower_o, balance_o,
    demand_v, avail_v, ptdf_v, limit_v, cost_v, cap_v, gnode_v, snode_v, power_v,
    capex_v, gen_v, store_v, upper_v, lower_v, flow_v, capacity_v,
    gen_w, store_w, capacity_w, flow_w, upper_w, lower_w,
    flow8, limit1, net_s, net_r, inj_s, inj_r, inj8, avail_d, demand_d,
    dual_s, dual_r, up_s, up_r, year_s, year_r, bar_s, bar_r, suffix_v, level_v,
    gbar_v, sbar_v, spread, onehot,
    in_sem, out_sem, net_sem, inj_sem, dual_sem, up_sem, year_sem, bar_sem,
):
    years_dev, hours_dev, hours, years, level_scale, node_scale, hour_count = sizes
    rows = years_dev * hours_dev
    me_h, me_y, me_l = lax.axis_index("hours"), lax.axis_index("years"), lax.axis_index("lines")
    nodes = ptdf_v.shape[1]
    hi_count = nodes // LANES
    line_local = ptdf_v.shape[0]
    gen_rows, store_rows = gnode_v.shape[0], snode_v.shape[0]
    link = dual_s.dtype

    order = (
        (upper_h, upper_v), (lower_h, lower_v), (snode_h, snode_v), (gnode_h, gnode_v),
        (flow_h, flow_v), (ptdf_h, ptdf_v), (store_h, store_v), (power_h, power_v),
        (gen_h, gen_v), (cost_h, cost_v), (cap_h, cap_v), (avail_h, avail_v),
        (demand_h, demand_v), (limit_h, limit_v), (capex_h, capex_v), (capacity_h, capacity_v),
    )
    loads = [pltpu.make_async_copy(s, d, in_sem.at[i]) for i, (s, d) in enumerate(order)]
    for copy in loads:
        copy.start()

    def hour_peer(k):
        return {"hours": lax.rem(me_h + k, hours)}

    def year_peer(k):
        return {"years": lax.rem(me_y + k, years)}

    partner = {"lines": 1 - me_l}
    barrier = pltpu.get_barrier_semaphore()
    peers = [partner] + [hour_peer(k) for k in range(1, hours)] + [year_peer(k) for k in range(1, years)]
    for peer in peers:
        pl.semaphore_signal(barrier, inc=1, device_id=peer, device_id_type=MESH)

    loads[0].wait()
    loads[1].wait()
    local_upper = None
    for y in range(years_dev):
        total = None
        for h in range(hours_dev):
            r = y * hours_dev + h
            diff = upper_v[r] - lower_v[r]
            total = diff if total is None else total + diff
            local_upper = upper_v[r] if local_upper is None else local_upper + upper_v[r]
        dual_s[y] = total.astype(link)
    up_s[...] = local_upper.astype(link)

    pl.semaphore_wait(barrier, len(peers))

    def remote(src, dst, sem, k, peer):
        return pltpu.make_async_remote_copy(
            src_ref=src, dst_ref=dst, send_sem=sem.at[0, k], recv_sem=sem.at[1, k],
            device_id=peer, device_id_type=MESH,
        )

    def dual_copy(k):
        return remote(dual_s, dual_r.at[k - 1], dual_sem, k - 1, hour_peer(hours - k))

    def bar_copy(k):
        return remote(bar_s, bar_r.at[k - 1], bar_sem, k - 1, hour_peer(k))

    ups = [remote(up_s, up_r.at[k - 1], up_sem, k - 1, hour_peer(k)) for k in range(1, hours)]
    year_copies = [remote(year_s, year_r.at[k - 1], year_sem, k - 1, year_peer(k)) for k in range(1, years)]
    net_copy = remote(net_s, net_r, net_sem, 0, partner)
    inj_copy = remote(inj_s, inj_r, inj_sem, 0, partner)

    for k in range(hours - 1, 0, -1):
        @pl.when(me_h >= k)
        def _(k=k):
            dual_copy(k).start()
    for copy in reversed(ups):
        copy.start()

    loads[2].wait()
    loads[3].wait()
    lane_rows = lax.broadcasted_iota(jnp.int32, (LANES, LANES), 0)

    def node_row(a):
        if a < store_rows:
            return snode_v[a : a + 1, :]
        return gnode_v[a - store_rows : a - store_rows + 1, :]

    for a in range(store_rows + gen_rows):
        low = jnp.broadcast_to(node_row(a) % LANES, (LANES, LANES))
        onehot[:, a * LANES : (a + 1) * LANES] = jnp.where(low == lane_rows, 1.0, 0.0).astype(jnp.bfloat16)

    loads[4].wait()
    flow8[...] = jnp.zeros_like(flow8)
    for r in range(rows):
        flow8[r : r + 1, :] = flow_v[r]
    dual_half = flow8[...].astype(jnp.bfloat16)
    loads[5].wait()
    net = jnp.dot(dual_half, ptdf_v[...], preferred_element_type=jnp.float32)
    net_s[...] = net[:rows]
    net_copy.start()

    for copy in loads[6:]:
        copy.wait()
    for y in range(years_dev):
        suffix_v[y] = jnp.zeros_like(suffix_v[y])
    for k in range(1, hours):
        @pl.when(me_h + k < hours)
        def _(k=k):
            dual_copy(k).wait_recv()
            for y in range(years_dev):
                suffix_v[y] = suffix_v[y] + dual_r[k - 1, y].astype(jnp.float32)
    for r in range(rows):
        for j in range(hi_count):
            piece = slice(j * LANES, (j + 1) * LANES)
            demand_d[r, j : j + 1, :] = demand_v[r : r + 1, piece].astype(jnp.float32)
        for j in range(gen_rows):
            piece = slice(j * LANES, (j + 1) * LANES)
            avail_d[r, j : j + 1, :] = avail_v[r : r + 1, piece].astype(jnp.float32)

    net_copy.wait_recv()
    prices = net_s[...] + net_r[...]

    def gather(r, node):
        price_row = prices[r : r + 1] + node_scale * balance_s[r]
        high, low = node // LANES, node % LANES
        result = jnp.zeros(node.shape, jnp.float32)
        for j in range(hi_count):
            table = jnp.broadcast_to(price_row[:, j * LANES : (j + 1) * LANES], node.shape)
            picked = jnp.take_along_axis(table, low, axis=1, mode="promise_in_bounds")
            result = jnp.where(high == j, picked, result)
        return result

    for y in range(years_dev):
        beyond = suffix_v[y]
        bar_total = jnp.zeros_like(beyond)
        for h in reversed(range(hours_dev)):
            r = y * hours_dev + h
            beyond = beyond + (upper_v[r] - lower_v[r])
            suffix = level_scale * beyond
            for b in range(0, store_rows, 8):
                part = slice(b, b + 8)
                price = gather(r, snode_v[part])
                power = power_v[part]
                new = store_v[r, part] - TAU * (suffix[part] - price)
                new = jnp.minimum(jnp.maximum(new, -power), power)
                store_w[r, part] = new
                sbar_v[r, part] = 2.0 * new - store_v[r, part]
            bar_total = bar_total + sbar_v[r]
        bar_s[y] = bar_total.astype(link)
    for k in range(hours - 1, 0, -1):
        @pl.when(me_h + k < hours)
        def _(k=k):
            bar_copy(k).start()
    outs = []

    def put(src, dst):
        copy = pltpu.make_async_copy(src, dst, out_sem.at[len(outs)])
        copy.start()
        outs.append(copy)

    put(store_w, store_o)
    for r in range(rows):
        for b in range(0, gen_rows, 8):
            part = slice(b, b + 8)
            price = gather(r, gnode_v[part])
            new = gen_v[r, part] - TAU * (cost_v[part] + price)
            new = jnp.minimum(jnp.maximum(new, 0.0), cap_v[part] * avail_d[r, part])
            gen_w[r, part] = new
            gbar_v[r, part] = 2.0 * new - gen_v[r, part]
    put(gen_w, gen_o)

    high_rows = lax.broadcasted_iota(jnp.int32, (hi_count, LANES), 0)
    for a in range(store_rows + gen_rows):
        hit = jnp.broadcast_to(node_row(a) // LANES, (hi_count, LANES)) == high_rows
        for r in range(rows):
            rest = -sbar_v[r, a : a + 1, :] if a < store_rows else gbar_v[r, a - store_rows : a - store_rows + 1, :]
            rest = jnp.where(hit, jnp.broadcast_to(rest, (hi_count, LANES)), 0.0)
            for p in range(SPLITS):
                piece = rest.astype(jnp.bfloat16)
                rest = rest - piece.astype(jnp.float32)
                base = (r * SPLITS + p) * hi_count
                spread[base : base + hi_count, a * LANES : (a + 1) * LANES] = piece
    placed = lax.dot_general(
        spread[...], onehot[...], (((1,), (1,)), ((), ())), preferred_element_type=jnp.float32
    )
    for r in range(rows):
        total = None
        for p in range(SPLITS):
            base = (r * SPLITS + p) * hi_count
            piece = placed[base : base + hi_count]
            total = piece if total is None else total + piece
        inj_s[r] = total
    inj_copy.start()

    for copy in ups:
        copy.wait_recv()
    upper_total = up_s[...].astype(jnp.float32)
    for k in range(1, hours):
        upper_total = upper_total + up_r[k - 1].astype(jnp.float32)
    year_s[...] = upper_total.astype(link)
    for copy in year_copies:
        copy.start()
    for c in range(line_local // LANES):
        limit1[:, c * LANES : (c + 1) * LANES] = limit_v[c : c + 1, :]
    inj8[...] = jnp.zeros_like(inj8)

    inj_copy.wait_recv()
    for r in range(rows):
        inject = inj_s[r] + inj_r[r] - demand_d[r]
        balance_o[r] = balance_s[r] + SIGMA * node_scale * jnp.sum(inject)
        for j in range(hi_count):
            inj8[r : r + 1, j * LANES : (j + 1) * LANES] = inject[j : j + 1]
    line_flows = lax.dot_general(
        inj8[...].astype(jnp.bfloat16), ptdf_v[...], (((1,), (1,)), ((), ())),
        preferred_element_type=jnp.float32,
    )
    shifted = flow8[...] + SIGMA * line_flows
    limit = limit1[...]
    line_next = shifted - SIGMA * jnp.minimum(jnp.maximum(shifted / SIGMA, -limit), limit)
    for r in range(rows):
        flow_w[r] = line_next[r : r + 1]
    put(flow_w, flow_o)

    for copy in year_copies:
        copy.wait_recv()
    for k in range(1, years):
        upper_total = upper_total + year_r[k - 1].astype(jnp.float32)
    capacity_next = jnp.maximum(capacity_v[...] - TAU_CAP * (capex_v[...] - upper_total / hour_count), 0.0)
    capacity_w[...] = capacity_next
    put(capacity_w, capacity_o)
    capacity_bar = 2.0 * capacity_next - capacity_v[...]

    for y in range(years_dev):
        level_v[y] = jnp.zeros_like(level_v[y])
    for k in range(1, hours):
        @pl.when(me_h >= k)
        def _(k=k):
            bar_copy(k).wait_recv()
            for y in range(years_dev):
                level_v[y] = level_v[y] + bar_r[k - 1, y].astype(jnp.float32)
    for y in range(years_dev):
        before = level_v[y]
        for h in range(hours_dev):
            r = y * hours_dev + h
            before = before + sbar_v[r]
            level = level_scale * before
            upper_w[r] = jnp.maximum(upper_v[r] + SIGMA * (level - capacity_bar), 0.0)
            lower_w[r] = jnp.maximum(lower_v[r] - SIGMA * level, 0.0)
    put(upper_w, upper_o)
    put(lower_w, lower_o)

    net_copy.wait_send()
    inj_copy.wait_send()
    for copy in ups + year_copies:
        copy.wait_send()
    for k in range(1, hours):
        @pl.when(me_h >= k)
        def _(k=k):
            dual_copy(k).wait_send()

        @pl.when(me_h + k < hours)
        def _(k=k):
            bar_copy(k).wait_send()
    for copy in outs:
        copy.wait()


def local(
    demand, avail, ptdf, line_limit, gen_cost, gen_cap, gen_node, store_node, store_power,
    capex, gen_state, store_state, level_upper, level_lower, flow_dual, balance_dual, capacity,
):
    years_dev, hours_dev, nodes = demand.shape
    rows = years_dev * hours_dev
    hours, years = lax.axis_size("hours"), lax.axis_size("years")
    hours_total = hours_dev * hours
    hour_count = years_dev * years * hours_total
    level_scale = 1.0 / math.sqrt(hours_total)
    node_scale = 1.0 / math.sqrt(nodes)
    sizes = (years_dev, hours_dev, hours, years, level_scale, node_scale, hour_count)

    def fold(x):
        return x.reshape(-1, LANES)

    def fold_rows(x):
        return x.reshape(rows, -1, LANES)

    args = (
        demand.reshape(rows, nodes), avail.reshape(rows, -1), ptdf, fold(line_limit), fold(gen_cost),
        fold(gen_cap), fold(gen_node), fold(store_node), fold(store_power), fold(capex),
        fold_rows(gen_state), fold_rows(store_state), fold_rows(level_upper), fold_rows(level_lower),
        flow_dual.reshape(rows, 1, -1), fold(capacity), balance_dual.reshape(rows),
    )
    f32 = jnp.float32
    gen_rows, store_rows = args[6].shape[0], args[7].shape[0]
    line_local, hi_count = ptdf.shape[0], nodes // LANES
    padded = max(8, -(-rows // 8) * 8)
    out_shapes = [
        (rows, gen_rows, LANES), (rows, store_rows, LANES), (store_rows, LANES),
        (rows, 1, line_local), (rows, store_rows, LANES), (rows, store_rows, LANES),
    ]
    any_spec = pl.BlockSpec(memory_space=pl.ANY)
    smem_spec = pl.BlockSpec(memory_space=pltpu.SMEM)
    block, blocks = (store_rows, LANES), (years_dev, store_rows, LANES)
    h1, y1 = max(hours - 1, 1), max(years - 1, 1)
    dma = pltpu.SemaphoreType.DMA
    scratch = [pltpu.VMEM(a.shape, a.dtype) for a in args[:16]]
    scratch += [pltpu.VMEM(s, f32) for s in out_shapes]
    scratch += [
        pltpu.VMEM((padded, line_local), f32), pltpu.VMEM((1, line_local), f32),
        pltpu.VMEM((rows, nodes), f32), pltpu.VMEM((rows, nodes), f32),
        pltpu.VMEM((rows, hi_count, LANES), f32), pltpu.VMEM((rows, hi_count, LANES), f32),
        pltpu.VMEM((padded, nodes), f32), pltpu.VMEM((rows, gen_rows, LANES), f32),
        pltpu.VMEM((rows, hi_count, LANES), f32),
        pltpu.VMEM(blocks, LINK), pltpu.VMEM((h1,) + blocks, LINK),
        pltpu.VMEM(block, LINK), pltpu.VMEM((h1,) + block, LINK),
        pltpu.VMEM(block, LINK), pltpu.VMEM((y1,) + block, LINK),
        pltpu.VMEM(blocks, LINK), pltpu.VMEM((h1,) + blocks, LINK),
        pltpu.VMEM(blocks, f32), pltpu.VMEM(blocks, f32),
        pltpu.VMEM((rows, gen_rows, LANES), f32), pltpu.VMEM((rows, store_rows, LANES), f32),
        pltpu.VMEM((rows * SPLITS * hi_count, (gen_rows + store_rows) * LANES), jnp.bfloat16),
        pltpu.VMEM((LANES, (gen_rows + store_rows) * LANES), jnp.bfloat16),
        dma((16,)), dma((6,)), dma((2, 1)), dma((2, 1)), dma((2, h1)), dma((2, h1)), dma((2, y1)), dma((2, h1)),
    ]
    results = pl.pallas_call(
        functools.partial(step_kernel, sizes),
        out_shape=[jax.ShapeDtypeStruct(s, f32) for s in out_shapes] + [jax.ShapeDtypeStruct((rows,), f32)],
        in_specs=[any_spec] * 16 + [smem_spec],
        out_specs=[any_spec] * 6 + [smem_spec],
        scratch_shapes=scratch,
        compiler_params=pltpu.CompilerParams(
            collective_id=0, has_side_effects=True, vmem_limit_bytes=56 * 1024 * 1024
        ),
    )(*args)
    gen, store, cap, flow, upper, lower, balance = results
    return (
        gen.reshape(gen_state.shape), store.reshape(store_state.shape), cap.reshape(capacity.shape),
        balance.reshape(balance_dual.shape), flow.reshape(flow_dual.shape),
        upper.reshape(level_upper.shape), lower.reshape(level_lower.shape),
    )


def solution(mesh):
    row = P(("groups", "years"), "hours", "lines")
    line = P("lines")
    in_specs = (
        P(("groups", "years"), "hours", None), row, P("lines", None), line, line, line, line, line,
        line, line, row, row, row, row, row, P(("groups", "years"), "hours"), P(("groups", "lines")),
    )
    out_specs = (row, row, P(("groups", "lines")), P(("groups", "years"), "hours"), row, row, row)
    return jax.shard_map(local, mesh=mesh, in_specs=in_specs, out_specs=out_specs, check_vma=False)
```

```python
import functools
import math

import jax
import jax.numpy as jnp
from jax import lax
from jax.experimental import pallas as pl
from jax.experimental.pallas import tpu as pltpu
from jax.sharding import PartitionSpec as P

TAU = 0.1
SIGMA = 0.5
TAU_CAP = 1.0
LANES = 128
SPLITS = 3
LINK = jnp.bfloat16
MESH = pl.DeviceIdType.MESH


def step_kernel(
    sizes,
    demand_h, avail_h, ptdf_h, limit_h, cost_h, cap_h, gnode_h, snode_h, power_h,
    capex_h, gen_h, store_h, upper_h, lower_h, flow_h, capacity_h, balance_h,
    gen_w, store_w, capacity_w, flow_w, upper_w, lower_w, balance_o,
    demand_v, avail_v, ptdf_v, limit_v, cost_v, cap_v, gnode_v, snode_v, power_v,
    capex_v, gen_v, store_v, upper_v, lower_v, flow_v, capacity_v, balance_v,
    flow8, limit1, net_s, net_r, inj_s, inj_r, inj8, avail_d, demand_d,
    dual_s, dual_r, up_s, up_r, year_s, year_r, bar_s, bar_r, suffix_v, level_v,
    gbar_v, sbar_v, price_v, spread, onehot,
    in_sem, net_sem, inj_sem, dual_sem, up_sem, year_sem, bar_sem,
):
    years_dev, hours_dev, hours, years, level_scale, node_scale, hour_count = sizes
    rows = years_dev * hours_dev
    me_h, me_y, me_l = lax.axis_index("hours"), lax.axis_index("years"), lax.axis_index("lines")
    nodes = ptdf_v.shape[1]
    hi_count = nodes // LANES
    line_local = ptdf_v.shape[0]
    gen_rows, store_rows = gnode_v.shape[0], snode_v.shape[0]
    link = dual_s.dtype

    order = (
        (upper_h, upper_v), (lower_h, lower_v), (snode_h, snode_v), (gnode_h, gnode_v),
        (flow_h, flow_v), (ptdf_h, ptdf_v), (store_h, store_v), (power_h, power_v),
        (gen_h, gen_v), (cost_h, cost_v), (cap_h, cap_v), (avail_h, avail_v),
        (demand_h, demand_v), (limit_h, limit_v), (capex_h, capex_v), (capacity_h, capacity_v),
        (balance_h, balance_v),
    )
    loads = [pltpu.make_async_copy(s, d, in_sem.at[i]) for i, (s, d) in enumerate(order)]

    def hour_peer(k):
        return {"hours": lax.rem(me_h + k, hours)}

    def year_peer(k):
        return {"years": lax.rem(me_y + k, years)}

    partner = {"lines": 1 - me_l}
    barrier = pltpu.get_barrier_semaphore()
    peers = [partner] + [hour_peer(k) for k in range(1, hours)] + [year_peer(k) for k in range(1, years)]
    for peer in peers:
        pl.semaphore_signal(barrier, inc=1, device_id=peer, device_id_type=MESH)
    for copy in loads:
        copy.start()

    loads[0].wait()
    loads[1].wait()
    local_upper = None
    for y in range(years_dev):
        total = None
        for h in range(hours_dev):
            r = y * hours_dev + h
            diff = upper_v[r] - lower_v[r]
            total = diff if total is None else total + diff
            local_upper = upper_v[r] if local_upper is None else local_upper + upper_v[r]
        dual_s[y] = total.astype(link)
    up_s[...] = local_upper

    pl.semaphore_wait(barrier, len(peers))

    def remote(src, dst, sem, k, peer):
        return pltpu.make_async_remote_copy(
            src_ref=src, dst_ref=dst, send_sem=sem.at[0, k], recv_sem=sem.at[1, k],
            device_id=peer, device_id_type=MESH,
        )

    def dual_copy(k):
        return remote(dual_s, dual_r.at[k - 1], dual_sem, k - 1, hour_peer(hours - k))

    def bar_copy(k):
        return remote(bar_s, bar_r.at[k - 1], bar_sem, k - 1, hour_peer(k))

    ups = [remote(up_s, up_r.at[k - 1], up_sem, k - 1, hour_peer(k)) for k in range(1, hours)]
    year_copies = [remote(year_s, year_r.at[k - 1], year_sem, k - 1, year_peer(k)) for k in range(1, years)]
    net_copy = remote(net_s, net_r, net_sem, 0, partner)
    inj_copy = remote(inj_s, inj_r, inj_sem, 0, partner)

    for k in range(hours - 1, 0, -1):
        @pl.when(me_h >= k)
        def _(k=k):
            dual_copy(k).start()

    loads[2].wait()
    loads[3].wait()
    lane_rows = lax.broadcasted_iota(jnp.int32, (LANES, LANES), 0)

    def node_row(a):
        if a < store_rows:
            return snode_v[a : a + 1, :]
        return gnode_v[a - store_rows : a - store_rows + 1, :]

    for a in range(store_rows + gen_rows):
        low = jnp.broadcast_to(node_row(a) % LANES, (LANES, LANES))
        onehot[:, a * LANES : (a + 1) * LANES] = jnp.where(low == lane_rows, 1.0, 0.0).astype(jnp.bfloat16)

    loads[4].wait()
    flow8[...] = jnp.zeros_like(flow8)
    for r in range(rows):
        flow8[r : r + 1, :] = flow_v[r]
    dual_half = flow8[...].astype(jnp.bfloat16)
    loads[5].wait()
    net = jnp.dot(dual_half, ptdf_v[...], preferred_element_type=jnp.float32)
    net_s[...] = net[:rows]
    net_copy.start()
    for copy in reversed(ups):
        copy.start()

    for copy in loads[6:]:
        copy.wait()
    for r in range(rows):
        for j in range(hi_count):
            piece = slice(j * LANES, (j + 1) * LANES)
            demand_d[r, j : j + 1, :] = demand_v[r : r + 1, piece].astype(jnp.float32)
        for j in range(gen_rows):
            piece = slice(j * LANES, (j + 1) * LANES)
            avail_d[r, j : j + 1, :] = avail_v[r : r + 1, piece].astype(jnp.float32)

    net_copy.wait_recv()
    prices = net_s[...] + net_r[...]

    def gather(r, node):
        price_row = prices[r : r + 1] + node_scale * balance_v[:, r : r + 1]
        high, low = node // LANES, node % LANES
        result = jnp.zeros(node.shape, jnp.float32)
        for j in range(hi_count):
            table = jnp.broadcast_to(price_row[:, j * LANES : (j + 1) * LANES], node.shape)
            picked = jnp.take_along_axis(table, low, axis=1, mode="promise_in_bounds")
            result = jnp.where(high == j, picked, result)
        return result

    for r in range(rows):
        for b in range(0, store_rows, 8):
            price_v[r, b : b + 8] = gather(r, snode_v[b : b + 8])

    for y in range(years_dev):
        suffix_v[y] = jnp.zeros_like(suffix_v[y])
    for k in range(1, hours):
        @pl.when(me_h + k < hours)
        def _(k=k):
            dual_copy(k).wait_recv()
            for y in range(years_dev):
                suffix_v[y] = suffix_v[y] + dual_r[k - 1, y].astype(jnp.float32)
    for y in range(years_dev):
        beyond = suffix_v[y]
        bar_total = jnp.zeros_like(beyond)
        for h in reversed(range(hours_dev)):
            r = y * hours_dev + h
            beyond = beyond + (upper_v[r] - lower_v[r])
            suffix = level_scale * beyond
            power = power_v[...]
            new = store_v[r] - TAU * (suffix - price_v[r])
            new = jnp.minimum(jnp.maximum(new, -power), power)
            store_w[r] = new
            sbar = 2.0 * new - store_v[r]
            sbar_v[r] = sbar
            bar_total = bar_total + sbar
        bar_s[y] = bar_total.astype(link)
    for k in range(hours - 1, 0, -1):
        @pl.when(me_h + k < hours)
        def _(k=k):
            bar_copy(k).start()
    for r in range(rows):
        for b in range(0, gen_rows, 8):
            part = slice(b, b + 8)
            price = gather(r, gnode_v[part])
            new = gen_v[r, part] - TAU * (cost_v[part] + price)
            new = jnp.minimum(jnp.maximum(new, 0.0), cap_v[part] * avail_d[r, part])
            gen_w[r, part] = new
            gbar_v[r, part] = 2.0 * new - gen_v[r, part]

    high_rows = lax.broadcasted_iota(jnp.int32, (hi_count, LANES), 0)
    for a in range(store_rows + gen_rows):
        hit = jnp.broadcast_to(node_row(a) // LANES, (hi_count, LANES)) == high_rows
        for r in range(rows):
            rest = -sbar_v[r, a : a + 1, :] if a < store_rows else gbar_v[r, a - store_rows : a - store_rows + 1, :]
            rest = jnp.where(hit, jnp.broadcast_to(rest, (hi_count, LANES)), 0.0)
            for p in range(SPLITS):
                piece = rest.astype(jnp.bfloat16)
                rest = rest - piece.astype(jnp.float32)
                base = (r * SPLITS + p) * hi_count
                spread[base : base + hi_count, a * LANES : (a + 1) * LANES] = piece
    placed = lax.dot_general(
        spread[...], onehot[...], (((1,), (1,)), ((), ())), preferred_element_type=jnp.float32
    )
    for r in range(rows):
        total = None
        for p in range(SPLITS):
            base = (r * SPLITS + p) * hi_count
            piece = placed[base : base + hi_count]
            total = piece if total is None else total + piece
        inj_s[r] = total
    inj_copy.start()

    for copy in ups:
        copy.wait_recv()
    upper_total = up_s[...]
    for k in range(1, hours):
        upper_total = upper_total + up_r[k - 1]
    year_s[...] = upper_total
    for copy in year_copies:
        copy.start()
    for c in range(line_local // LANES):
        limit1[:, c * LANES : (c + 1) * LANES] = limit_v[c : c + 1, :]
    inj8[...] = jnp.zeros_like(inj8)

    inj_copy.wait_recv()
    for r in range(rows):
        inject = inj_s[r] + inj_r[r] - demand_d[r]
        balance_o[:, r : r + 1] = balance_v[:, r : r + 1] + SIGMA * node_scale * jnp.sum(inject, keepdims=True)
        for j in range(hi_count):
            inj8[r : r + 1, j * LANES : (j + 1) * LANES] = inject[j : j + 1]
    line_flows = lax.dot_general(
        inj8[...].astype(jnp.bfloat16), ptdf_v[...], (((1,), (1,)), ((), ())),
        preferred_element_type=jnp.float32,
    )
    shifted = flow8[...] + SIGMA * line_flows
    limit = limit1[...]
    line_next = shifted - SIGMA * jnp.minimum(jnp.maximum(shifted / SIGMA, -limit), limit)
    for r in range(rows):
        flow_w[r] = line_next[r : r + 1]

    for copy in year_copies:
        copy.wait_recv()
    for k in range(1, years):
        upper_total = upper_total + year_r[k - 1]
    capacity_next = jnp.maximum(capacity_v[...] - TAU_CAP * (capex_v[...] - upper_total / hour_count), 0.0)
    capacity_w[...] = capacity_next
    capacity_bar = 2.0 * capacity_next - capacity_v[...]

    for y in range(years_dev):
        level_v[y] = jnp.zeros_like(level_v[y])
    for k in range(1, hours):
        @pl.when(me_h >= k)
        def _(k=k):
            bar_copy(k).wait_recv()
            for y in range(years_dev):
                level_v[y] = level_v[y] + bar_r[k - 1, y].astype(jnp.float32)
    for y in range(years_dev):
        before = level_v[y]
        for h in range(hours_dev):
            r = y * hours_dev + h
            before = before + sbar_v[r]
            level = level_scale * before
            upper_w[r] = jnp.maximum(upper_v[r] + SIGMA * (level - capacity_bar), 0.0)
            lower_w[r] = jnp.maximum(lower_v[r] - SIGMA * level, 0.0)

    net_copy.wait_send()
    inj_copy.wait_send()
    for copy in ups + year_copies:
        copy.wait_send()
    for k in range(1, hours):
        @pl.when(me_h >= k)
        def _(k=k):
            dual_copy(k).wait_send()

        @pl.when(me_h + k < hours)
        def _(k=k):
            bar_copy(k).wait_send()


def finish_kernel(count, *refs):
    sources, targets, sem = refs[:count], refs[count : 2 * count], refs[2 * count]
    copies = [pltpu.make_async_copy(s, t, sem.at[i]) for i, (s, t) in enumerate(zip(sources, targets))]
    for copy in copies:
        copy.start()
    for copy in copies:
        copy.wait()


def local(
    demand, avail, ptdf, line_limit, gen_cost, gen_cap, gen_node, store_node, store_power,
    capex, gen_state, store_state, level_upper, level_lower, flow_dual, balance_dual, capacity,
):
    years_dev, hours_dev, nodes = demand.shape
    rows = years_dev * hours_dev
    hours, years = lax.axis_size("hours"), lax.axis_size("years")
    hours_total = hours_dev * hours
    hour_count = years_dev * years * hours_total
    level_scale = 1.0 / math.sqrt(hours_total)
    node_scale = 1.0 / math.sqrt(nodes)
    sizes = (years_dev, hours_dev, hours, years, level_scale, node_scale, hour_count)

    def fold(x):
        return x.reshape(-1, LANES)

    def fold_rows(x):
        return x.reshape(rows, -1, LANES)

    args = (
        demand.reshape(rows, nodes), avail.reshape(rows, -1), ptdf, fold(line_limit), fold(gen_cost),
        fold(gen_cap), fold(gen_node), fold(store_node), fold(store_power), fold(capex),
        fold_rows(gen_state), fold_rows(store_state), fold_rows(level_upper), fold_rows(level_lower),
        flow_dual.reshape(rows, 1, -1), fold(capacity), balance_dual.reshape(1, rows),
    )
    f32 = jnp.float32
    gen_rows, store_rows = args[6].shape[0], args[7].shape[0]
    line_local, hi_count = ptdf.shape[0], nodes // LANES
    padded = max(8, -(-rows // 8) * 8)
    out_shapes = [
        (rows, gen_rows, LANES), (rows, store_rows, LANES), (store_rows, LANES),
        (rows, 1, line_local), (rows, store_rows, LANES), (rows, store_rows, LANES),
    ]
    any_spec = pl.BlockSpec(memory_space=pl.ANY)
    block, blocks = (store_rows, LANES), (years_dev, store_rows, LANES)
    h1, y1 = max(hours - 1, 1), max(years - 1, 1)
    dma = pltpu.SemaphoreType.DMA
    scratch = [pltpu.VMEM(a.shape, a.dtype) for a in args]
    scratch += [
        pltpu.VMEM((padded, line_local), f32), pltpu.VMEM((1, line_local), f32),
        pltpu.VMEM((rows, nodes), f32), pltpu.VMEM((rows, nodes), f32),
        pltpu.VMEM((rows, hi_count, LANES), f32), pltpu.VMEM((rows, hi_count, LANES), f32),
        pltpu.VMEM((padded, nodes), f32), pltpu.VMEM((rows, gen_rows, LANES), f32),
        pltpu.VMEM((rows, hi_count, LANES), f32),
        pltpu.VMEM(blocks, LINK), pltpu.VMEM((h1,) + blocks, LINK),
        pltpu.VMEM(block, f32), pltpu.VMEM((h1,) + block, f32),
        pltpu.VMEM(block, f32), pltpu.VMEM((y1,) + block, f32),
        pltpu.VMEM(blocks, LINK), pltpu.VMEM((h1,) + blocks, LINK),
        pltpu.VMEM(blocks, f32), pltpu.VMEM(blocks, f32),
        pltpu.VMEM((rows, gen_rows, LANES), f32), pltpu.VMEM((rows, store_rows, LANES), f32),
        pltpu.VMEM((rows, store_rows, LANES), f32),
        pltpu.VMEM((rows * SPLITS * hi_count, (gen_rows + store_rows) * LANES), jnp.bfloat16),
        pltpu.VMEM((LANES, (gen_rows + store_rows) * LANES), jnp.bfloat16),
        dma((17,)), dma((2, 1)), dma((2, 1)), dma((2, h1)), dma((2, h1)), dma((2, y1)), dma((2, h1)),
    ]
    results = pl.pallas_call(
        functools.partial(step_kernel, sizes),
        out_shape=[jax.ShapeDtypeStruct(s, f32) for s in out_shapes] + [jax.ShapeDtypeStruct((1, rows), f32)],
        in_specs=[any_spec] * 17,
        out_specs=[pl.BlockSpec(memory_space=pltpu.VMEM)] * 7,
        scratch_shapes=scratch,
        compiler_params=pltpu.CompilerParams(
            collective_id=0, has_side_effects=True, vmem_limit_bytes=62 * 1024 * 1024
        ),
    )(*args)
    gen, store, cap, flow, upper, lower, balance = pl.pallas_call(
        functools.partial(finish_kernel, len(results)),
        out_shape=[jax.ShapeDtypeStruct(x.shape, f32) for x in results],
        in_specs=[any_spec] * len(results),
        out_specs=[any_spec] * len(results),
        scratch_shapes=[dma((len(results),))],
    )(*results)
    return (
        gen.reshape(gen_state.shape), store.reshape(store_state.shape), cap.reshape(capacity.shape),
        balance.reshape(balance_dual.shape), flow.reshape(flow_dual.shape),
        upper.reshape(level_upper.shape), lower.reshape(level_lower.shape),
    )


def solution(mesh):
    row = P(("groups", "years"), "hours", "lines")
    line = P("lines")
    in_specs = (
        P(("groups", "years"), "hours", None), row, P("lines", None), line, line, line, line, line,
        line, line, row, row, row, row, row, P(("groups", "years"), "hours"), P(("groups", "lines")),
    )
    out_specs = (row, row, P(("groups", "lines")), P(("groups", "years"), "hours"), row, row, row)
    return jax.shard_map(local, mesh=mesh, in_specs=in_specs, out_specs=out_specs, check_vma=False)
```

```python
import functools
import math

import jax
import jax.numpy as jnp
from jax import lax
from jax.experimental import pallas as pl
from jax.experimental.pallas import tpu as pltpu
from jax.sharding import PartitionSpec as P

TAU = 0.1
SIGMA = 0.5
TAU_CAP = 1.0
LANES = 128
SPLITS = 2
LINK = jnp.bfloat16
MESH = pl.DeviceIdType.MESH


def step_kernel(
    sizes,
    demand_h, avail_h, ptdf_h, limit_h, cost_h, cap_h, gnode_h, snode_h, power_h,
    capex_h, gen_h, store_h, upper_h, lower_h, flow_h, capacity_h, balance_h,
    gen_w, store_w, capacity_w, flow_w, upper_w, lower_w, balance_o,
    demand_v, avail_v, ptdf_v, limit_v, cost_v, cap_v, gnode_v, snode_v, power_v,
    capex_v, gen_v, store_v, upper_v, lower_v, flow_v, capacity_v, balance_v,
    flow8, limit1, net_s, net_r, inj_s, inj_r, inj8, avail_d, demand_d,
    dual_s, dual_r, up_s, up_r, year_s, year_r, bar_s, bar_r, suffix_v, level_v,
    gbar_v, sbar_v, price_v, spread, onehot, highhot,
    in_sem, net_sem, inj_sem, dual_sem, up_sem, year_sem, bar_sem,
):
    years_dev, hours_dev, hours, years, level_scale, node_scale, hour_count = sizes
    rows = years_dev * hours_dev
    me_h, me_y, me_l = lax.axis_index("hours"), lax.axis_index("years"), lax.axis_index("lines")
    nodes = ptdf_v.shape[1]
    hi_count = nodes // LANES
    line_local = ptdf_v.shape[0]
    gen_rows, store_rows = gnode_v.shape[0], snode_v.shape[0]
    link = dual_s.dtype

    order = (
        (upper_h, upper_v), (lower_h, lower_v), (snode_h, snode_v), (gnode_h, gnode_v),
        (flow_h, flow_v), (ptdf_h, ptdf_v), (store_h, store_v), (power_h, power_v),
        (gen_h, gen_v), (cost_h, cost_v), (cap_h, cap_v), (avail_h, avail_v),
        (demand_h, demand_v), (limit_h, limit_v), (capex_h, capex_v), (capacity_h, capacity_v),
        (balance_h, balance_v),
    )
    loads = [pltpu.make_async_copy(s, d, in_sem.at[i]) for i, (s, d) in enumerate(order)]

    def hour_peer(k):
        return {"hours": lax.rem(me_h + k, hours)}

    def year_peer(k):
        return {"years": lax.rem(me_y + k, years)}

    partner = {"lines": 1 - me_l}
    barrier = pltpu.get_barrier_semaphore()
    peers = [partner] + [hour_peer(k) for k in range(1, hours)] + [year_peer(k) for k in range(1, years)]
    for peer in peers:
        pl.semaphore_signal(barrier, inc=1, device_id=peer, device_id_type=MESH)
    for copy in loads:
        copy.start()

    loads[0].wait()
    loads[1].wait()
    local_upper = None
    for y in range(years_dev):
        total = None
        for h in range(hours_dev):
            r = y * hours_dev + h
            diff = upper_v[r] - lower_v[r]
            total = diff if total is None else total + diff
            local_upper = upper_v[r] if local_upper is None else local_upper + upper_v[r]
        dual_s[y] = total.astype(link)
    year_s[...] = local_upper

    pl.semaphore_wait(barrier, len(peers))

    def remote(src, dst, sem, k, peer):
        return pltpu.make_async_remote_copy(
            src_ref=src, dst_ref=dst, send_sem=sem.at[0, k], recv_sem=sem.at[1, k],
            device_id=peer, device_id_type=MESH,
        )

    def dual_copy(k):
        return remote(dual_s, dual_r.at[k - 1], dual_sem, k - 1, hour_peer(hours - k))

    def bar_copy(k):
        return remote(bar_s, bar_r.at[k - 1], bar_sem, k - 1, hour_peer(k))

    ups = [remote(up_s, up_r.at[k - 1], up_sem, k - 1, hour_peer(k)) for k in range(1, hours)]
    year_copies = [remote(year_s, year_r.at[k - 1], year_sem, k - 1, year_peer(k)) for k in range(1, years)]
    net_copy = remote(net_s, net_r, net_sem, 0, partner)
    inj_copy = remote(inj_s, inj_r, inj_sem, 0, partner)

    for k in range(hours - 1, 0, -1):
        @pl.when(me_h >= k)
        def _(k=k):
            dual_copy(k).start()
    for copy in year_copies:
        copy.start()

    loads[2].wait()
    loads[3].wait()
    high_rows = lax.broadcasted_iota(jnp.int32, (hi_count, LANES), 0)
    lane_rows = lax.broadcasted_iota(jnp.int32, (LANES, LANES), 0)

    def node_row(a):
        if a < store_rows:
            return snode_v[a : a + 1, :]
        return gnode_v[a - store_rows : a - store_rows + 1, :]

    for a in range(store_rows + gen_rows):
        low = jnp.broadcast_to(node_row(a) % LANES, (LANES, LANES))
        onehot[:, a * LANES : (a + 1) * LANES] = jnp.where(low == lane_rows, 1.0, 0.0).astype(jnp.bfloat16)
        high = jnp.broadcast_to(node_row(a) // LANES, (hi_count, LANES))
        highhot[:, a * LANES : (a + 1) * LANES] = jnp.where(high == high_rows, 1.0, 0.0).astype(jnp.bfloat16)

    for copy in year_copies:
        copy.wait_recv()
    block_upper = year_s[...]
    for k in range(1, years):
        block_upper = block_upper + year_r[k - 1]
    up_s[...] = block_upper
    for copy in reversed(ups):
        copy.start()

    loads[4].wait()
    flow8[...] = jnp.zeros_like(flow8)
    for r in range(rows):
        flow8[r : r + 1, :] = flow_v[r]
    dual_half = flow8[...].astype(jnp.bfloat16)
    loads[5].wait()
    net = jnp.dot(dual_half, ptdf_v[...], preferred_element_type=jnp.float32)
    net_s[...] = net[:rows]
    net_copy.start()

    for copy in loads[6:]:
        copy.wait()
    for r in range(rows):
        for j in range(hi_count):
            piece = slice(j * LANES, (j + 1) * LANES)
            demand_d[r, j : j + 1, :] = demand_v[r : r + 1, piece].astype(jnp.float32)
        for j in range(gen_rows):
            piece = slice(j * LANES, (j + 1) * LANES)
            avail_d[r, j : j + 1, :] = avail_v[r : r + 1, piece].astype(jnp.float32)

    net_copy.wait_recv()
    prices = net_s[...] + net_r[...]

    def gather(r, node):
        price_row = prices[r : r + 1] + node_scale * balance_v[:, r : r + 1]
        high, low = node // LANES, node % LANES
        result = jnp.zeros(node.shape, jnp.float32)
        for j in range(hi_count):
            table = jnp.broadcast_to(price_row[:, j * LANES : (j + 1) * LANES], node.shape)
            picked = jnp.take_along_axis(table, low, axis=1, mode="promise_in_bounds")
            result = jnp.where(high == j, picked, result)
        return result

    for r in range(rows):
        for b in range(0, store_rows, 8):
            price_v[r, b : b + 8] = gather(r, snode_v[b : b + 8])

    for r in range(rows):
        for b in range(0, gen_rows, 8):
            part = slice(b, b + 8)
            price = gather(r, gnode_v[part])
            new = gen_v[r, part] - TAU * (cost_v[part] + price)
            new = jnp.minimum(jnp.maximum(new, 0.0), cap_v[part] * avail_d[r, part])
            gen_w[r, part] = new
            gbar_v[r, part] = 2.0 * new - gen_v[r, part]

    def place(values, sign, first, count):
        for r in range(rows):
            rest = sign * values[r]
            for p in range(SPLITS):
                piece = rest.astype(jnp.bfloat16).astype(jnp.float32)
                rest = rest - piece
                base = (r * SPLITS + p) * hi_count
                for a in range(count):
                    cols = slice((first + a) * LANES, (first + a + 1) * LANES)
                    wide = jnp.broadcast_to(piece[a : a + 1], (hi_count, LANES)).astype(jnp.bfloat16)
                    spread[base : base + hi_count, cols] = wide * highhot[:, cols]
        cols = slice(first * LANES, (first + count) * LANES)
        return lax.dot_general(
            spread[:, cols], onehot[:, cols], (((1,), (1,)), ((), ())), preferred_element_type=jnp.float32
        )

    placed = place(gbar_v, 1.0, store_rows, gen_rows)

    for y in range(years_dev):
        suffix_v[y] = jnp.zeros_like(suffix_v[y])
    for k in range(1, hours):
        @pl.when(me_h + k < hours)
        def _(k=k):
            dual_copy(k).wait_recv()
            for y in range(years_dev):
                suffix_v[y] = suffix_v[y] + dual_r[k - 1, y].astype(jnp.float32)
    for y in range(years_dev):
        beyond = suffix_v[y]
        bar_total = jnp.zeros_like(beyond)
        for h in reversed(range(hours_dev)):
            r = y * hours_dev + h
            beyond = beyond + (upper_v[r] - lower_v[r])
            suffix = level_scale * beyond
            power = power_v[...]
            new = store_v[r] - TAU * (suffix - price_v[r])
            new = jnp.minimum(jnp.maximum(new, -power), power)
            store_w[r] = new
            sbar = 2.0 * new - store_v[r]
            sbar_v[r] = sbar
            bar_total = bar_total + sbar
        bar_s[y] = bar_total.astype(link)
    for k in range(hours - 1, 0, -1):
        @pl.when(me_h + k < hours)
        def _(k=k):
            bar_copy(k).start()
    placed = placed + place(sbar_v, -1.0, 0, store_rows)
    for r in range(rows):
        total = None
        for p in range(SPLITS):
            base = (r * SPLITS + p) * hi_count
            piece = placed[base : base + hi_count]
            total = piece if total is None else total + piece
        inj_s[r] = total
    inj_copy.start()

    for c in range(line_local // LANES):
        limit1[:, c * LANES : (c + 1) * LANES] = limit_v[c : c + 1, :]
    inj8[...] = jnp.zeros_like(inj8)

    inj_copy.wait_recv()
    for r in range(rows):
        inject = inj_s[r] + inj_r[r] - demand_d[r]
        balance_o[:, r : r + 1] = balance_v[:, r : r + 1] + SIGMA * node_scale * jnp.sum(inject, keepdims=True)
        for j in range(hi_count):
            inj8[r : r + 1, j * LANES : (j + 1) * LANES] = inject[j : j + 1]
    line_flows = lax.dot_general(
        inj8[...].astype(jnp.bfloat16), ptdf_v[...], (((1,), (1,)), ((), ())),
        preferred_element_type=jnp.float32,
    )
    shifted = flow8[...] + SIGMA * line_flows
    limit = limit1[...]
    line_next = shifted - SIGMA * jnp.minimum(jnp.maximum(shifted / SIGMA, -limit), limit)
    for r in range(rows):
        flow_w[r] = line_next[r : r + 1]

    for copy in ups:
        copy.wait_recv()
    upper_total = up_s[...]
    for k in range(1, hours):
        upper_total = upper_total + up_r[k - 1]
    capacity_next = jnp.maximum(capacity_v[...] - TAU_CAP * (capex_v[...] - upper_total / hour_count), 0.0)
    capacity_w[...] = capacity_next
    capacity_bar = 2.0 * capacity_next - capacity_v[...]

    for y in range(years_dev):
        level_v[y] = jnp.zeros_like(level_v[y])
    for k in range(1, hours):
        @pl.when(me_h >= k)
        def _(k=k):
            bar_copy(k).wait_recv()
            for y in range(years_dev):
                level_v[y] = level_v[y] + bar_r[k - 1, y].astype(jnp.float32)
    for y in range(years_dev):
        before = level_v[y]
        for h in range(hours_dev):
            r = y * hours_dev + h
            before = before + sbar_v[r]
            level = level_scale * before
            upper_w[r] = jnp.maximum(upper_v[r] + SIGMA * (level - capacity_bar), 0.0)
            lower_w[r] = jnp.maximum(lower_v[r] - SIGMA * level, 0.0)

    net_copy.wait_send()
    inj_copy.wait_send()
    for copy in ups + year_copies:
        copy.wait_send()
    for k in range(1, hours):
        @pl.when(me_h >= k)
        def _(k=k):
            dual_copy(k).wait_send()

        @pl.when(me_h + k < hours)
        def _(k=k):
            bar_copy(k).wait_send()


def finish_kernel(count, *refs):
    sources, targets, sem = refs[:count], refs[count : 2 * count], refs[2 * count]
    copies = [pltpu.make_async_copy(s, t, sem.at[i]) for i, (s, t) in enumerate(zip(sources, targets))]
    for copy in copies:
        copy.start()
    for copy in copies:
        copy.wait()


def local(
    demand, avail, ptdf, line_limit, gen_cost, gen_cap, gen_node, store_node, store_power,
    capex, gen_state, store_state, level_upper, level_lower, flow_dual, balance_dual, capacity,
):
    years_dev, hours_dev, nodes = demand.shape
    rows = years_dev * hours_dev
    hours, years = lax.axis_size("hours"), lax.axis_size("years")
    hours_total = hours_dev * hours
    hour_count = years_dev * years * hours_total
    level_scale = 1.0 / math.sqrt(hours_total)
    node_scale = 1.0 / math.sqrt(nodes)
    sizes = (years_dev, hours_dev, hours, years, level_scale, node_scale, hour_count)

    def fold(x):
        return x.reshape(-1, LANES)

    def fold_rows(x):
        return x.reshape(rows, -1, LANES)

    args = (
        demand.reshape(rows, nodes), avail.reshape(rows, -1), ptdf, fold(line_limit), fold(gen_cost),
        fold(gen_cap), fold(gen_node), fold(store_node), fold(store_power), fold(capex),
        fold_rows(gen_state), fold_rows(store_state), fold_rows(level_upper), fold_rows(level_lower),
        flow_dual.reshape(rows, 1, -1), fold(capacity), balance_dual.reshape(1, rows),
    )
    f32 = jnp.float32
    gen_rows, store_rows = args[6].shape[0], args[7].shape[0]
    line_local, hi_count = ptdf.shape[0], nodes // LANES
    padded = max(8, -(-rows // 8) * 8)
    out_shapes = [
        (rows, gen_rows, LANES), (rows, store_rows, LANES), (store_rows, LANES),
        (rows, 1, line_local), (rows, store_rows, LANES), (rows, store_rows, LANES),
    ]
    any_spec = pl.BlockSpec(memory_space=pl.ANY)
    block, blocks = (store_rows, LANES), (years_dev, store_rows, LANES)
    h1, y1 = max(hours - 1, 1), max(years - 1, 1)
    dma = pltpu.SemaphoreType.DMA
    scratch = [pltpu.VMEM(a.shape, a.dtype) for a in args]
    scratch += [
        pltpu.VMEM((padded, line_local), f32), pltpu.VMEM((1, line_local), f32),
        pltpu.VMEM((rows, nodes), f32), pltpu.VMEM((rows, nodes), f32),
        pltpu.VMEM((rows, hi_count, LANES), f32), pltpu.VMEM((rows, hi_count, LANES), f32),
        pltpu.VMEM((padded, nodes), f32), pltpu.VMEM((rows, gen_rows, LANES), f32),
        pltpu.VMEM((rows, hi_count, LANES), f32),
        pltpu.VMEM(blocks, LINK), pltpu.VMEM((h1,) + blocks, LINK),
        pltpu.VMEM(block, f32), pltpu.VMEM((h1,) + block, f32),
        pltpu.VMEM(block, f32), pltpu.VMEM((y1,) + block, f32),
        pltpu.VMEM(blocks, LINK), pltpu.VMEM((h1,) + blocks, LINK),
        pltpu.VMEM(blocks, f32), pltpu.VMEM(blocks, f32),
        pltpu.VMEM((rows, gen_rows, LANES), f32), pltpu.VMEM((rows, store_rows, LANES), f32),
        pltpu.VMEM((rows, store_rows, LANES), f32),
        pltpu.VMEM((rows * SPLITS * hi_count, (gen_rows + store_rows) * LANES), jnp.bfloat16),
        pltpu.VMEM((LANES, (gen_rows + store_rows) * LANES), jnp.bfloat16),
        pltpu.VMEM((hi_count, (gen_rows + store_rows) * LANES), jnp.bfloat16),
        dma((17,)), dma((2, 1)), dma((2, 1)), dma((2, h1)), dma((2, h1)), dma((2, y1)), dma((2, h1)),
    ]
    results = pl.pallas_call(
        functools.partial(step_kernel, sizes),
        out_shape=[pltpu.VMEM(s, f32) for s in out_shapes] + [pltpu.VMEM((1, rows), f32)],
        in_specs=[any_spec] * 17,
        out_specs=[pl.BlockSpec(memory_space=pltpu.VMEM)] * 7,
        scratch_shapes=scratch,
        compiler_params=pltpu.CompilerParams(
            collective_id=0, has_side_effects=True, vmem_limit_bytes=56 * 1024 * 1024
        ),
    )(*args)
    gen, store, cap, flow, upper, lower, balance = pl.pallas_call(
        functools.partial(finish_kernel, len(results)),
        out_shape=[jax.ShapeDtypeStruct(x.shape, f32) for x in results],
        in_specs=[pl.BlockSpec(memory_space=pltpu.VMEM)] * len(results),
        out_specs=[any_spec] * len(results),
        scratch_shapes=[dma((len(results),))],
    )(*[pltpu.with_memory_space_constraint(x, pltpu.VMEM) for x in results])
    return (
        gen.reshape(gen_state.shape), store.reshape(store_state.shape), cap.reshape(capacity.shape),
        balance.reshape(balance_dual.shape), flow.reshape(flow_dual.shape),
        upper.reshape(level_upper.shape), lower.reshape(level_lower.shape),
    )


def solution(mesh):
    row = P(("groups", "years"), "hours", "lines")
    line = P("lines")
    in_specs = (
        P(("groups", "years"), "hours", None), row, P("lines", None), line, line, line, line, line,
        line, line, row, row, row, row, row, P(("groups", "years"), "hours"), P(("groups", "lines")),
    )
    out_specs = (row, row, P(("groups", "lines")), P(("groups", "years"), "hours"), row, row, row)
    return jax.shard_map(local, mesh=mesh, in_specs=in_specs, out_specs=out_specs, check_vma=False)
```

```python
import functools
import math

import jax
import jax.numpy as jnp
from jax import lax
from jax.experimental import pallas as pl
from jax.experimental.pallas import tpu as pltpu
from jax.sharding import PartitionSpec as P

TAU = 0.1
SIGMA = 0.5
TAU_CAP = 1.0
LANES = 128
SPLITS = 2
LINK = jnp.bfloat16
MESH = pl.DeviceIdType.MESH


def step_kernel(
    sizes,
    demand_h, avail_h, ptdf_h, limit_h, cost_h, cap_h, gnode_h, snode_h, power_h,
    capex_h, gen_h, store_h, upper_h, lower_h, flow_h, capacity_h, balance_h,
    gen_w, store_w, capacity_w, flow_w, upper_w, lower_w, balance_o,
    demand_v, avail_v, ptdf_v, limit_v, cost_v, cap_v, gnode_v, snode_v, power_v,
    capex_v, gen_v, store_v, upper_v, lower_v, flow_v, capacity_v, balance_v,
    flow8, limit1, net_s, net_r, inj_s, inj_r, inj8, avail_d, demand_d,
    dual_s, dual_r, up_s, up_r, year_s, year_r, bar_s, bar_r, suffix_v, level_v,
    gbar_v, sbar_v, price_v, spread, onehot, highhot,
    in_sem, net_sem, inj_sem, dual_sem, up_sem, year_sem, bar_sem,
):
    years_dev, hours_dev, hours, years, level_scale, node_scale, hour_count = sizes
    rows = years_dev * hours_dev
    me_h, me_y, me_l = lax.axis_index("hours"), lax.axis_index("years"), lax.axis_index("lines")
    nodes = ptdf_v.shape[1]
    hi_count = nodes // LANES
    line_local = ptdf_v.shape[0]
    gen_rows, store_rows = gnode_v.shape[0], snode_v.shape[0]
    link = dual_s.dtype

    order = (
        (upper_h, upper_v), (lower_h, lower_v), (snode_h, snode_v), (gnode_h, gnode_v),
        (flow_h, flow_v), (ptdf_h, ptdf_v), (store_h, store_v), (power_h, power_v),
        (gen_h, gen_v), (cost_h, cost_v), (cap_h, cap_v), (avail_h, avail_v),
        (demand_h, demand_v), (limit_h, limit_v), (capex_h, capex_v), (capacity_h, capacity_v),
        (balance_h, balance_v),
    )
    loads = [pltpu.make_async_copy(s, d, in_sem.at[i]) for i, (s, d) in enumerate(order)]

    def hour_peer(k):
        return {"hours": lax.rem(me_h + k, hours)}

    def year_peer(k):
        return {"years": lax.rem(me_y + k, years)}

    partner = {"lines": 1 - me_l}
    barrier = pltpu.get_barrier_semaphore()
    peers = [partner] + [hour_peer(k) for k in range(1, hours)] + [year_peer(k) for k in range(1, years)]
    for peer in peers:
        pl.semaphore_signal(barrier, inc=1, device_id=peer, device_id_type=MESH)
    for copy in loads:
        copy.start()

    loads[0].wait()
    loads[1].wait()
    local_upper = None
    for y in range(years_dev):
        total = None
        for h in range(hours_dev):
            r = y * hours_dev + h
            diff = upper_v[r] - lower_v[r]
            total = diff if total is None else total + diff
            local_upper = upper_v[r] if local_upper is None else local_upper + upper_v[r]
        dual_s[y] = total.astype(link)
    year_s[...] = local_upper

    pl.semaphore_wait(barrier, len(peers))

    def remote(src, dst, sem, k, peer):
        return pltpu.make_async_remote_copy(
            src_ref=src, dst_ref=dst, send_sem=sem.at[0, k], recv_sem=sem.at[1, k],
            device_id=peer, device_id_type=MESH,
        )

    def dual_copy(k):
        return remote(dual_s, dual_r.at[k - 1], dual_sem, k - 1, hour_peer(hours - k))

    def bar_copy(k):
        return remote(bar_s, bar_r.at[k - 1], bar_sem, k - 1, hour_peer(k))

    ups = [remote(up_s, up_r.at[k - 1], up_sem, k - 1, hour_peer(k)) for k in range(1, hours)]
    year_copies = [remote(year_s, year_r.at[k - 1], year_sem, k - 1, year_peer(k)) for k in range(1, years)]
    net_copy = remote(net_s, net_r, net_sem, 0, partner)
    inj_copy = remote(inj_s, inj_r, inj_sem, 0, partner)

    for k in range(hours - 1, 0, -1):
        @pl.when(me_h >= k)
        def _(k=k):
            dual_copy(k).start()
    for copy in year_copies:
        copy.start()

    loads[4].wait()
    flow8[...] = jnp.zeros_like(flow8)
    for r in range(rows):
        flow8[r : r + 1, :] = flow_v[r]
    dual_half = flow8[...].astype(jnp.bfloat16)
    loads[5].wait()
    net = jnp.dot(dual_half, ptdf_v[...], preferred_element_type=jnp.float32)
    net_s[...] = net[:rows]
    net_copy.start()

    for copy in year_copies:
        copy.wait_recv()
    block_upper = year_s[...]
    for k in range(1, years):
        block_upper = block_upper + year_r[k - 1]
    up_s[...] = block_upper
    for copy in reversed(ups):
        copy.start()

    loads[2].wait()
    loads[3].wait()
    high_rows = lax.broadcasted_iota(jnp.int32, (hi_count, LANES), 0)
    lane_rows = lax.broadcasted_iota(jnp.int32, (LANES, LANES), 0)

    def node_row(a):
        if a < store_rows:
            return snode_v[a : a + 1, :]
        return gnode_v[a - store_rows : a - store_rows + 1, :]

    for a in range(store_rows + gen_rows):
        low = jnp.broadcast_to(node_row(a) % LANES, (LANES, LANES))
        onehot[:, a * LANES : (a + 1) * LANES] = jnp.where(low == lane_rows, 1.0, 0.0).astype(jnp.bfloat16)
        high = jnp.broadcast_to(node_row(a) // LANES, (hi_count, LANES))
        highhot[:, a * LANES : (a + 1) * LANES] = jnp.where(high == high_rows, 1.0, 0.0).astype(jnp.bfloat16)

    for copy in loads[6:]:
        copy.wait()
    for r in range(rows):
        for j in range(hi_count):
            piece = slice(j * LANES, (j + 1) * LANES)
            demand_d[r, j : j + 1, :] = demand_v[r : r + 1, piece].astype(jnp.float32)
        for j in range(gen_rows):
            piece = slice(j * LANES, (j + 1) * LANES)
            avail_d[r, j : j + 1, :] = avail_v[r : r + 1, piece].astype(jnp.float32)

    net_copy.wait_recv()
    prices = net_s[...] + net_r[...]

    def gather(r, node):
        price_row = prices[r : r + 1] + node_scale * balance_v[:, r : r + 1]
        high, low = node // LANES, node % LANES
        result = jnp.zeros(node.shape, jnp.float32)
        for j in range(hi_count):
            table = jnp.broadcast_to(price_row[:, j * LANES : (j + 1) * LANES], node.shape)
            picked = jnp.take_along_axis(table, low, axis=1, mode="promise_in_bounds")
            result = jnp.where(high == j, picked, result)
        return result

    for r in range(rows):
        for b in range(0, store_rows, 8):
            price_v[r, b : b + 8] = gather(r, snode_v[b : b + 8])

    for r in range(rows):
        for b in range(0, gen_rows, 8):
            part = slice(b, b + 8)
            price = gather(r, gnode_v[part])
            new = gen_v[r, part] - TAU * (cost_v[part] + price)
            new = jnp.minimum(jnp.maximum(new, 0.0), cap_v[part] * avail_d[r, part])
            gen_w[r, part] = new
            gbar_v[r, part] = 2.0 * new - gen_v[r, part]

    def place(values, sign, first, count):
        for r in range(rows):
            rest = sign * values[r]
            for p in range(SPLITS):
                piece = rest.astype(jnp.bfloat16).astype(jnp.float32)
                rest = rest - piece
                base = (r * SPLITS + p) * hi_count
                for a in range(count):
                    cols = slice((first + a) * LANES, (first + a + 1) * LANES)
                    wide = jnp.broadcast_to(piece[a : a + 1], (hi_count, LANES)).astype(jnp.bfloat16)
                    spread[base : base + hi_count, cols] = wide * highhot[:, cols]
        cols = slice(first * LANES, (first + count) * LANES)
        return lax.dot_general(
            spread[:, cols], onehot[:, cols], (((1,), (1,)), ((), ())), preferred_element_type=jnp.float32
        )

    placed = place(gbar_v, 1.0, store_rows, gen_rows)

    for y in range(years_dev):
        suffix_v[y] = jnp.zeros_like(suffix_v[y])
    for k in range(1, hours):
        @pl.when(me_h + k < hours)
        def _(k=k):
            dual_copy(k).wait_recv()
            for y in range(years_dev):
                suffix_v[y] = suffix_v[y] + dual_r[k - 1, y].astype(jnp.float32)
    for y in range(years_dev):
        beyond = suffix_v[y]
        bar_total = jnp.zeros_like(beyond)
        for h in reversed(range(hours_dev)):
            r = y * hours_dev + h
            beyond = beyond + (upper_v[r] - lower_v[r])
            suffix = level_scale * beyond
            power = power_v[...]
            new = store_v[r] - TAU * (suffix - price_v[r])
            new = jnp.minimum(jnp.maximum(new, -power), power)
            store_w[r] = new
            sbar = 2.0 * new - store_v[r]
            sbar_v[r] = sbar
            bar_total = bar_total + sbar
        bar_s[y] = bar_total.astype(link)
    for k in range(hours - 1, 0, -1):
        @pl.when(me_h + k < hours)
        def _(k=k):
            bar_copy(k).start()
    placed = placed + place(sbar_v, -1.0, 0, store_rows)
    for r in range(rows):
        total = None
        for p in range(SPLITS):
            base = (r * SPLITS + p) * hi_count
            piece = placed[base : base + hi_count]
            total = piece if total is None else total + piece
        inj_s[r] = total
    inj_copy.start()

    for c in range(line_local // LANES):
        limit1[:, c * LANES : (c + 1) * LANES] = limit_v[c : c + 1, :]
    inj8[...] = jnp.zeros_like(inj8)

    inj_copy.wait_recv()
    for r in range(rows):
        inject = inj_s[r] + inj_r[r] - demand_d[r]
        balance_o[:, r : r + 1] = balance_v[:, r : r + 1] + SIGMA * node_scale * jnp.sum(inject, keepdims=True)
        for j in range(hi_count):
            inj8[r : r + 1, j * LANES : (j + 1) * LANES] = inject[j : j + 1]
    line_flows = lax.dot_general(
        inj8[...].astype(jnp.bfloat16), ptdf_v[...], (((1,), (1,)), ((), ())),
        preferred_element_type=jnp.float32,
    )
    shifted = flow8[...] + SIGMA * line_flows
    limit = limit1[...]
    line_next = shifted - SIGMA * jnp.minimum(jnp.maximum(shifted / SIGMA, -limit), limit)
    for r in range(rows):
        flow_w[r] = line_next[r : r + 1]

    for copy in ups:
        copy.wait_recv()
    upper_total = up_s[...]
    for k in range(1, hours):
        upper_total = upper_total + up_r[k - 1]
    capacity_next = jnp.maximum(capacity_v[...] - TAU_CAP * (capex_v[...] - upper_total / hour_count), 0.0)
    capacity_w[...] = capacity_next
    capacity_bar = 2.0 * capacity_next - capacity_v[...]

    for y in range(years_dev):
        level_v[y] = jnp.zeros_like(level_v[y])
    for k in range(1, hours):
        @pl.when(me_h >= k)
        def _(k=k):
            bar_copy(k).wait_recv()
            for y in range(years_dev):
                level_v[y] = level_v[y] + bar_r[k - 1, y].astype(jnp.float32)
    for y in range(years_dev):
        before = level_v[y]
        for h in range(hours_dev):
            r = y * hours_dev + h
            before = before + sbar_v[r]
            level = level_scale * before
            upper_w[r] = jnp.maximum(upper_v[r] + SIGMA * (level - capacity_bar), 0.0)
            lower_w[r] = jnp.maximum(lower_v[r] - SIGMA * level, 0.0)

    net_copy.wait_send()
    inj_copy.wait_send()
    for copy in ups + year_copies:
        copy.wait_send()
    for k in range(1, hours):
        @pl.when(me_h >= k)
        def _(k=k):
            dual_copy(k).wait_send()

        @pl.when(me_h + k < hours)
        def _(k=k):
            bar_copy(k).wait_send()


def finish_kernel(count, *refs):
    sources, targets, sem = refs[:count], refs[count : 2 * count], refs[2 * count]
    copies = [pltpu.make_async_copy(s, t, sem.at[i]) for i, (s, t) in enumerate(zip(sources, targets))]
    for copy in copies:
        copy.start()
    for copy in copies:
        copy.wait()


def local(
    demand, avail, ptdf, line_limit, gen_cost, gen_cap, gen_node, store_node, store_power,
    capex, gen_state, store_state, level_upper, level_lower, flow_dual, balance_dual, capacity,
):
    years_dev, hours_dev, nodes = demand.shape
    rows = years_dev * hours_dev
    hours, years = lax.axis_size("hours"), lax.axis_size("years")
    hours_total = hours_dev * hours
    hour_count = years_dev * years * hours_total
    level_scale = 1.0 / math.sqrt(hours_total)
    node_scale = 1.0 / math.sqrt(nodes)
    sizes = (years_dev, hours_dev, hours, years, level_scale, node_scale, hour_count)

    def fold(x):
        return x.reshape(-1, LANES)

    def fold_rows(x):
        return x.reshape(rows, -1, LANES)

    args = (
        demand.reshape(rows, nodes), avail.reshape(rows, -1), ptdf, fold(line_limit), fold(gen_cost),
        fold(gen_cap), fold(gen_node), fold(store_node), fold(store_power), fold(capex),
        fold_rows(gen_state), fold_rows(store_state), fold_rows(level_upper), fold_rows(level_lower),
        flow_dual.reshape(rows, 1, -1), fold(capacity), balance_dual.reshape(1, rows),
    )
    f32 = jnp.float32
    gen_rows, store_rows = args[6].shape[0], args[7].shape[0]
    line_local, hi_count = ptdf.shape[0], nodes // LANES
    padded = max(8, -(-rows // 8) * 8)
    out_shapes = [
        (rows, gen_rows, LANES), (rows, store_rows, LANES), (store_rows, LANES),
        (rows, 1, line_local), (rows, store_rows, LANES), (rows, store_rows, LANES),
    ]
    any_spec = pl.BlockSpec(memory_space=pl.ANY)
    block, blocks = (store_rows, LANES), (years_dev, store_rows, LANES)
    h1, y1 = max(hours - 1, 1), max(years - 1, 1)
    dma = pltpu.SemaphoreType.DMA
    scratch = [pltpu.VMEM(a.shape, a.dtype) for a in args]
    scratch += [
        pltpu.VMEM((padded, line_local), f32), pltpu.VMEM((1, line_local), f32),
        pltpu.VMEM((rows, nodes), f32), pltpu.VMEM((rows, nodes), f32),
        pltpu.VMEM((rows, hi_count, LANES), f32), pltpu.VMEM((rows, hi_count, LANES), f32),
        pltpu.VMEM((padded, nodes), f32), pltpu.VMEM((rows, gen_rows, LANES), f32),
        pltpu.VMEM((rows, hi_count, LANES), f32),
        pltpu.VMEM(blocks, LINK), pltpu.VMEM((h1,) + blocks, LINK),
        pltpu.VMEM(block, f32), pltpu.VMEM((h1,) + block, f32),
        pltpu.VMEM(block, f32), pltpu.VMEM((y1,) + block, f32),
        pltpu.VMEM(blocks, LINK), pltpu.VMEM((h1,) + blocks, LINK),
        pltpu.VMEM(blocks, f32), pltpu.VMEM(blocks, f32),
        pltpu.VMEM((rows, gen_rows, LANES), f32), pltpu.VMEM((rows, store_rows, LANES), f32),
        pltpu.VMEM((rows, store_rows, LANES), f32),
        pltpu.VMEM((rows * SPLITS * hi_count, (gen_rows + store_rows) * LANES), jnp.bfloat16),
        pltpu.VMEM((LANES, (gen_rows + store_rows) * LANES), jnp.bfloat16),
        pltpu.VMEM((hi_count, (gen_rows + store_rows) * LANES), jnp.bfloat16),
        dma((17,)), dma((2, 1)), dma((2, 1)), dma((2, h1)), dma((2, h1)), dma((2, y1)), dma((2, h1)),
    ]
    results = pl.pallas_call(
        functools.partial(step_kernel, sizes),
        out_shape=[pltpu.VMEM(s, f32) for s in out_shapes] + [pltpu.VMEM((1, rows), f32)],
        in_specs=[any_spec] * 17,
        out_specs=[pl.BlockSpec(memory_space=pltpu.VMEM)] * 7,
        scratch_shapes=scratch,
        compiler_params=pltpu.CompilerParams(
            collective_id=0, has_side_effects=True, vmem_limit_bytes=56 * 1024 * 1024
        ),
    )(*args)
    gen, store, cap, flow, upper, lower, balance = pl.pallas_call(
        functools.partial(finish_kernel, len(results)),
        out_shape=[jax.ShapeDtypeStruct(x.shape, f32) for x in results],
        in_specs=[pl.BlockSpec(memory_space=pltpu.VMEM)] * len(results),
        out_specs=[any_spec] * len(results),
        scratch_shapes=[dma((len(results),))],
    )(*[pltpu.with_memory_space_constraint(x, pltpu.VMEM) for x in results])
    return (
        gen.reshape(gen_state.shape), store.reshape(store_state.shape), cap.reshape(capacity.shape),
        balance.reshape(balance_dual.shape), flow.reshape(flow_dual.shape),
        upper.reshape(level_upper.shape), lower.reshape(level_lower.shape),
    )


def solution(mesh):
    row = P(("groups", "years"), "hours", "lines")
    line = P("lines")
    in_specs = (
        P(("groups", "years"), "hours", None), row, P("lines", None), line, line, line, line, line,
        line, line, row, row, row, row, row, P(("groups", "years"), "hours"), P(("groups", "lines")),
    )
    out_specs = (row, row, P(("groups", "lines")), P(("groups", "years"), "hours"), row, row, row)
    return jax.shard_map(local, mesh=mesh, in_specs=in_specs, out_specs=out_specs, check_vma=False)
```
